32 devices in a mesh: blk: 8 (over z, x), rep: 4 (over y, core).
Axes of the slice: x: 2, y: 2, z: 4, core: 2. Of those that a mesh axis runs over, the one named last changes fastest.
Arguments:
- a_blocks: bfloat16 [24, 8, 6, 128, 128], P('blk', None, None, None, 'rep'), may hold values from -0.5 to 0.5
- a_cols: int32 [24, 8, 6], P('blk'), may hold values from 0 to 111, as said below
- b_blocks: bfloat16 [896, 4, 3, 128, 128], P('blk', 'rep'), may hold values from -6 to 6
- b_cols: int32 [896, 4, 3], P('blk', 'rep'), may hold values from 0 to 223, as said below
- c_cols: int32 [24, 4, 4], P(None, 'rep'), may hold values from 0 to 223, as said below
Outputs:
- c_blocks: float32 [24, 4, 4, 128, 128], P('blk', 'rep')
The draws below stay inside these ranges and needn't reach their ends.
Inputs may be any that keep to these rules, and one draw needn't show every extreme that they name: `a_cols`: within each block row and panel the 6 entries are distinct. `b_cols`: within each block row and tile the 3 entries are distinct. `c_cols`: within each block row and tile the 4 entries are distinct.
All inputs are finite; a program needn't handle non-finite values.
Results may differ from the reference program's by a relative error of at most 0.0003.
Values may be sent and summed in bfloat16 or wider, within the bound.
No kernel may reach another device: no remote copies, remote signals or barrier semaphores. Data moves between devices by JAX's collectives and lax.ppermute only.
A program may use at most 128 MiB of HBM per device.

```python
import jax
import jax.numpy as jnp
from jax import lax

BS = 128
KP = 112
KA = 6
KB = 3
KC = 4
PANELS = 8
TILES = 4
NROW = 24
NB = 896
CT = 224


def distinct_lists(key, rows, middle, pool, count):
    scores = jax.random.randint(key, (rows, middle, pool), 0, 65536) * pool + jnp.arange(pool, dtype=jnp.int32)
    order = jnp.argsort(scores, axis=-1)[:, :, :count].astype(jnp.int32)
    order = order.at[0, 0].set(pool - 1 - jnp.arange(count, dtype=jnp.int32))
    order = order.at[1, 0].set(jnp.arange(count, dtype=jnp.int32))
    return order


def draw_a_cols(key, part):
    return distinct_lists(jax.random.fold_in(key, 11), NROW, PANELS, KP, KA)


def pick_window(key, salt, rows, count):
    span = 2 * max(KB, KC)
    base = jax.random.fold_in(key, 0)
    offsets = jax.random.randint(jax.random.fold_in(base, 99), (TILES,), 0, CT - span + 1).astype(jnp.int32)
    scores = jax.random.randint(jax.random.fold_in(base, salt), (rows, TILES, span), 0, 65536) * span + jnp.arange(span, dtype=jnp.int32)
    order = jnp.argsort(scores, axis=-1)[:, :, :count].astype(jnp.int32) + offsets[None, :, None]
    order = order.at[0, 0].set(CT - 1 - jnp.arange(count, dtype=jnp.int32))
    order = order.at[1, 0].set(jnp.arange(count, dtype=jnp.int32))
    return order.astype(jnp.int32)


def draw_b_cols(key, part):
    return pick_window(key, 23, NB, KB)


def draw_c_cols(key, part):
    return pick_window(key, 37, NROW, KC)


def block_scale(stream_key, shape, cuts, low, top_value):
    gain, own = 1.0, jax.random.fold_in(stream_key, 6)
    for dim, blocks in cuts:
        draws = jnp.exp(jax.random.uniform(jax.random.fold_in(own, dim), (blocks,), jnp.float32, low / len(cuts), top_value / len(cuts)))
        gain = gain * jnp.repeat(draws, shape[dim] // blocks).reshape([-1 if axis == dim else 1 for axis in range(len(shape))])
    return gain


def scatter_about(stream_key, extent, scale, reach, shards=(), kind=jnp.bfloat16):
    result = scale * jax.random.normal(stream_key, extent, jnp.float32)
    if shards:
        result = result * block_scale(stream_key, extent, shards, -0.22, 0.18)
    return jnp.clip(result, -reach, reach).astype(kind)


def setup_inputs(seed: int = 0) -> dict:
    splits = jax.random.split(jax.random.key(seed), 6)
    a_blocks = scatter_about(splits[0], (NROW, PANELS, KA, BS, BS), BS ** -0.5, 0.5, ((0, 8), (4, 4)))
    a_cols = draw_a_cols(jax.random.fold_in(splits[5], 71), 0)
    b_blocks = scatter_about(splits[2], (NB, TILES, KB, BS, BS), 1.0, 6.0, ((0, 8), (1, 4)))
    b_cols = draw_b_cols(jax.random.fold_in(splits[5], 71), 0)
    c_cols = draw_c_cols(jax.random.fold_in(splits[5], 71), 0)
    return dict(a_blocks=a_blocks, a_cols=a_cols, b_blocks=b_blocks, b_cols=b_cols, c_cols=c_cols)


def reference(a_blocks, a_cols, b_blocks, b_cols, c_cols):
    panel_base = (jnp.arange(PANELS, dtype=jnp.int32) * KP)[:, None]
    slots = PANELS * KA

    def one_row(items):
        a_row, cols_row, pattern_row = items
        global_k = (cols_row.astype(jnp.int32) + panel_base).reshape(slots).astype(jnp.int32)
        chosen = b_blocks[global_k]
        chosen_cols = b_cols[global_k]
        hits = chosen_cols[:, :, :, None] == pattern_row[None, :, None, :]
        picked = jnp.zeros((slots, TILES, KC, BS, BS), b_blocks.dtype)
        for slot_t in range(KB):
            picked = picked + jnp.where(hits[:, :, slot_t, :, None, None], chosen[:, :, slot_t, None], jnp.zeros((), b_blocks.dtype))
        left = a_row.reshape(slots, BS, BS).astype(jnp.float32)
        return jnp.einsum("sab,srcbd->rcad", left, picked.astype(jnp.float32))

    return lax.map(one_row, (a_blocks, a_cols, c_cols))
```

```python
import functools

import jax
import jax.numpy as jnp
from jax import lax
from jax.experimental import pallas as pl
from jax.experimental.pallas import tpu as pltpu
from jax.sharding import PartitionSpec as P


LEVELS = 32600.0
STEPS = 256.0
TAIL = 16
VMEM_LIMIT = 60 * 1024 * 1024


def split_two(extent):
    inner = 2 if extent % 2 == 0 else 1
    return extent // inner, inner


def partner(index, step, extent):
    return index ^ step if extent & (extent - 1) == 0 else (index + step) % extent


def source(index, step, extent):
    return index ^ step if extent & (extent - 1) == 0 else (index + extent - step) % extent


def routes(extent, step, flip):
    outer, inner = split_two(extent)
    return [
        (o * inner + i, partner(o, step, outer) * inner + (i ^ flip))
        for o in range(outer)
        for i in range(inner)
    ]


def back_routes(extent, step):
    return [(to, frm) for frm, to in routes(extent, step, 0)]


def encode(values):
    top = jnp.max(jnp.abs(values), axis=0, keepdims=True)
    code = jnp.ceil(jnp.log2(jnp.maximum(top, 1e-33)) * STEPS)
    factor = jnp.exp2(code * (-1.0 / STEPS)) * LEVELS
    return jnp.round(values * factor).astype(jnp.int32).astype(jnp.int16), code


def store_codes(out_ref, row, column, values, codes):
    size = values.shape[1]
    coded, code = encode(values)
    out_ref[row, pl.ds(column * size, size), :] = coded
    line = lax.broadcasted_iota(jnp.int32, (TAIL, size), 0)
    return jnp.where(line == column, code, codes)


def decode(ref, row, column, codes):
    size = codes.shape[1]
    step = jnp.exp2(codes[column : column + 1] * (1.0 / STEPS)) * (1.0 / LEVELS)
    return ref[row, pl.ds(column * size, size), :].astype(jnp.int32).astype(jnp.float32) * step


def scales(ref, row, per):
    size = ref.shape[2]
    return ref[row, pl.ds(per * size, TAIL), :].astype(jnp.int32).astype(jnp.float32)


def product_kernel(first, own, slots, held, per, size, coded, pieces, tab_ref, b_ref, *refs):
    piece_refs, out_ref = refs[:pieces], refs[pieces]
    left_ref, right_ref, piece_sem, block_sem = refs[pieces + 1 :]
    width = piece_refs[0].shape[2]
    last = own * slots * held

    def block_copy(row, slot):
        n = row * slots + slot
        return pltpu.make_async_copy(
            b_ref.at[tab_ref[first + row, slot]],
            right_ref.at[pl.ds(n * held, held)],
            block_sem.at[n],
        )

    def piece_copy(n):
        at = pl.multiple_of(tab_ref[tab_ref.shape[0] - 1, n] * width, width)
        return pltpu.make_async_copy(
            piece_refs[n], left_ref.at[:, :, pl.ds(at, width), :], piece_sem.at[n]
        )

    for row in range(own):
        for slot in range(slots):
            block_copy(row, slot).start()
    for n in range(pieces):
        piece_copy(n).start()
    right_ref[last] = jnp.zeros((size, size), right_ref.dtype)
    for n in range(pieces):
        piece_copy(n).wait()

    for row in range(own):
        for slot in range(slots):
            block_copy(row, slot).wait()
        codes = jnp.zeros((TAIL, size), jnp.float32)
        for c0 in range(0, per, 2):
            columns = range(c0, min(c0 + 2, per))
            total = None
            for s0 in range(0, slots, 2):
                span = range(s0, min(s0 + 2, slots))
                left = left_ref[row, pl.ds(s0, len(span))].reshape(len(span) * size, size)
                right = jnp.concatenate(
                    [
                        jnp.concatenate(
                            [right_ref[tab_ref[first + row, slots + s * per + c]] for c in columns],
                            axis=1,
                        )
                        for s in span
                    ],
                    axis=0,
                )
                term = lax.dot_general(
                    left, right, (((0,), (0,)), ((), ())), preferred_element_type=jnp.float32
                )
                total = term if total is None else total + term
            for c in columns:
                value = total[:, (c - c0) * size : (c - c0 + 1) * size]
                if coded:
                    codes = store_codes(out_ref, row, c, value, codes)
                else:
                    out_ref[row, c] = value
        if coded:
            out_ref[row, pl.ds(per * size, TAIL), :] = codes.astype(jnp.int32).astype(jnp.int16)


def product(tab, local_b, pieces, first, own, per, coded):
    slots, size = pieces[0].shape[1], pieces[0].shape[3]
    held = local_b.shape[1]
    if coded:
        out = jax.ShapeDtypeStruct((own, per * size + TAIL, size), jnp.int16)
    else:
        out = jax.ShapeDtypeStruct((own, per, size, size), jnp.float32)
    return pl.pallas_call(
        functools.partial(
            product_kernel, first, own, slots, held, per, size, coded, len(pieces)
        ),
        out_shape=out,
        in_specs=[pl.BlockSpec(memory_space=pltpu.SMEM)]
        + [pl.BlockSpec(memory_space=pl.ANY)] * (1 + len(pieces)),
        out_specs=pl.BlockSpec(memory_space=pltpu.VMEM),
        scratch_shapes=[
            pltpu.VMEM((own, slots, size, size), local_b.dtype),
            pltpu.VMEM((own * slots * held + 1, size, size), local_b.dtype),
            pltpu.SemaphoreType.DMA((len(pieces),)),
            pltpu.SemaphoreType.DMA((own * slots,)),
        ],
        compiler_params=pltpu.CompilerParams(vmem_limit_bytes=VMEM_LIMIT),
        cost_estimate=pl.CostEstimate(
            flops=2 * own * slots * per * size**3,
            bytes_accessed=own * slots * (held + 1) * size * size * 2 + own * per * size * size * 4,
            transcendentals=0,
        ),
        name="product_coded" if coded else "product_kept",
    )(tab, local_b, *pieces)


def sum_kernel(per, size, coded, kept_ref, *refs):
    coded_refs, out_ref = refs[:-1], refs[-1]
    codes_in = [scales(ref, 0, per) for ref in coded_refs]
    codes = jnp.zeros((TAIL, size), jnp.float32)
    for c in range(per):
        value = kept_ref[0, c]
        for ref, code in zip(coded_refs, codes_in, strict=True):
            value = value + decode(ref, 0, c, code)
        if coded:
            codes = store_codes(out_ref, 0, c, value, codes)
        else:
            out_ref[0, c] = value
    if coded:
        out_ref[0, pl.ds(per * size, TAIL), :] = codes.astype(jnp.int32).astype(jnp.int16)


def combine(kept, arrived, coded):
    own, per, size, _ = kept.shape
    rows = per * size + TAIL
    kept_spec = pl.BlockSpec((1, per, size, size), lambda r: (r, 0, 0, 0))
    coded_spec = pl.BlockSpec((1, rows, size), lambda r: (r, 0, 0))
    out = jax.ShapeDtypeStruct((own, rows, size), jnp.int16) if coded else kept
    return pl.pallas_call(
        functools.partial(sum_kernel, per, size, coded),
        grid=(own,),
        out_shape=jax.ShapeDtypeStruct(out.shape, out.dtype),
        in_specs=[kept_spec] + [coded_spec] * len(arrived),
        out_specs=coded_spec if coded else kept_spec,
        compiler_params=pltpu.CompilerParams(vmem_limit_bytes=VMEM_LIMIT),
        cost_estimate=pl.CostEstimate(
            flops=own * rows * size * 4,
            bytes_accessed=own * rows * size * (4 + 2 * len(arrived) + 2),
            transcendentals=0,
        ),
        name="sum_coded" if coded else "sum_kept",
    )(kept, *arrived)


def gather_pieces(piece):
    extent = lax.axis_size("rep")
    outer, inner = split_two(extent)
    pieces = [piece]
    for step in range(1, outer):
        pieces.append(lax.ppermute(piece, "rep", routes(extent, step, 0)))
    if inner == 2:
        pieces += [lax.ppermute(p, "rep", routes(extent, 0, 1)) for p in pieces]
    return pieces


def piece_order():
    extent = lax.axis_size("rep")
    outer, inner = split_two(extent)
    me = lax.axis_index("rep")
    o, i = me // inner, me % inner
    return [
        source(o, step, outer) * inner + (i ^ flip) for flip in range(inner) for step in range(outer)
    ]


def per_device(a_blocks, a_cols, b_blocks, b_cols, c_cols):
    own, panels, slots, size, width = a_blocks.shape
    local_b, local_bcols, pattern = b_blocks[:, 0], b_cols[:, 0], c_cols[:, 0]
    held, per = local_b.shape[1], pattern.shape[1]
    extent = lax.axis_size("blk")
    outer, inner = split_two(extent)
    me = lax.axis_index("blk")
    o, i = me // inner, me % inner
    a_turned = jnp.swapaxes(a_blocks, 3, 4)

    def take_panel(panel):
        return lax.dynamic_index_in_dim(a_turned, panel, 1, keepdims=False)

    steps = list(range(1, outer))[::-1] + [0]
    order = [(k, j) for k in steps for j in reversed(range(inner))]

    arrived = {}
    for k, j in [(0, j) for j in reversed(range(inner))] + [x for x in order if x[0]]:
        sent = take_panel(partner(o, k, outer) * inner + (i ^ j))
        arrived[k, j] = lax.ppermute(sent, "blk", routes(extent, k, j)) if k or j else sent

    slab_cols = lax.all_to_all(a_cols, "blk", split_axis=1, concat_axis=0, tiled=True)
    where_k = slab_cols.reshape(extent * own, slots)
    hits = local_bcols[where_k][:, :, :, None] == pattern[:, None, None, :]
    slot_t = jnp.arange(held, dtype=jnp.int32)[None, None, :, None]
    found = jnp.min(jnp.where(hits, slot_t, held), axis=2)
    line = (jnp.arange(extent * own, dtype=jnp.int32) % own)[:, None, None]
    at = (line * slots + jnp.arange(slots, dtype=jnp.int32)[None, :, None]) * held + found
    at = jnp.where(found < held, at, own * slots * held)
    table = jnp.concatenate([where_k, at.reshape(extent * own, slots * per)], axis=1)
    owners = jnp.stack([source(o, k, outer) * inner + (i ^ j) for k, j in order])
    table = table.reshape(extent, own, -1)[owners].reshape(extent * own, -1)
    places = piece_order()
    columns = max(table.shape[1], len(places))
    table = jnp.pad(table, ((0, 1), (0, columns - table.shape[1])))
    table = table.at[-1, : len(places)].set(jnp.stack(places).astype(jnp.int32))

    def ready(k, j):
        if width % 16 == 0:
            return gather_pieces(arrived[k, j])
        return [lax.all_gather(arrived[k, j], "rep", axis=2, tiled=True)]

    final, kept_own = [], None
    for k in steps:
        kept, over = None, []
        for j in reversed(range(inner)):
            done = product(
                table, local_b, ready(k, j), order.index((k, j)) * own, own, per, coded=j > 0
            )
            if j:
                over.append(lax.ppermute(done, "blk", routes(extent, 0, j)))
            else:
                kept = done
        if k:
            summed = combine(kept, over, coded=True)
            final.append(lax.ppermute(summed, "blk", back_routes(extent, k)))
        else:
            kept_own = kept
            final += over
    mine = combine(kept_own, final, coded=False)
    return mine.reshape(own, 1, per, size, size)


def solution(mesh):
    placed = (
        P("blk", None, None, None, "rep"),
        P("blk", None, None),
        P("blk", "rep", None, None, None),
        P("blk", "rep", None),
        P(None, "rep", None),
    )
    return jax.shard_map(
        per_device,
        mesh=mesh,
        in_specs=placed,
        out_specs=P("blk", "rep", None, None, None),
        check_vma=False,
    )
```

```python
import functools

import jax
import jax.numpy as jnp
from jax import lax
from jax.experimental import pallas as pl
from jax.experimental.pallas import tpu as pltpu
from jax.sharding import PartitionSpec as P


LEVELS = 32600.0
STEPS = 256.0
TAIL = 16
VMEM_LIMIT = 12 * 1024 * 1024


def split_two(extent):
    inner = 2 if extent % 2 == 0 else 1
    return extent // inner, inner


def partner(index, step, extent):
    return index ^ step if extent & (extent - 1) == 0 else (index + step) % extent


def source(index, step, extent):
    return index ^ step if extent & (extent - 1) == 0 else (index + extent - step) % extent


def routes(extent, step, flip):
    outer, inner = split_two(extent)
    return [
        (o * inner + i, partner(o, step, outer) * inner + (i ^ flip))
        for o in range(outer)
        for i in range(inner)
    ]


def back_routes(extent, step):
    return [(to, frm) for frm, to in routes(extent, step, 0)]


def hop(step, extent):
    return step & -step if extent & (extent - 1) == 0 else step


def encode(values):
    top = jnp.max(jnp.abs(values), axis=0, keepdims=True)
    code = jnp.ceil(jnp.log2(jnp.maximum(top, 1e-33)) * STEPS)
    factor = jnp.exp2(code * (-1.0 / STEPS)) * LEVELS
    return jnp.round(values * factor).astype(jnp.int32).astype(jnp.int16), code


def store_codes(out_ref, row, column, values, codes):
    size = values.shape[1]
    coded, code = encode(values)
    out_ref[row, pl.ds(column * size, size), :] = coded
    line = lax.broadcasted_iota(jnp.int32, (TAIL, size), 0)
    return jnp.where(line == column, code, codes)


def decode(ref, row, column, codes):
    size = codes.shape[1]
    step = jnp.exp2(codes[column : column + 1] * (1.0 / STEPS)) * (1.0 / LEVELS)
    return ref[row, pl.ds(column * size, size), :].astype(jnp.int32).astype(jnp.float32) * step


def scales(ref, row, per):
    size = ref.shape[2]
    return ref[row, pl.ds(per * size, TAIL), :].astype(jnp.int32).astype(jnp.float32)


def product_kernel(first, own, slots, per, size, coded, pieces, tab_ref, b_ref, *refs):
    piece_refs, out_ref, left_ref = refs[:pieces], refs[pieces], refs[pieces + 1]
    width = piece_refs[0].shape[2]

    for n in range(pieces):
        at = pl.multiple_of(tab_ref[tab_ref.shape[0] - 1, n] * width, width)
        left_ref[:, :, pl.ds(at, width), :] = piece_refs[n][...]

    def block(row, s, c):
        at = tab_ref[first + row, slots + s * per + c]
        found = b_ref[jnp.maximum(at, 0)]
        return jnp.where(at >= 0, found, jnp.zeros_like(found))

    for row in range(own):
        codes = jnp.zeros((TAIL, size), jnp.float32)
        lefts = []
        for s0 in range(0, slots, 2):
            span = range(s0, min(s0 + 2, slots))
            lefts.append((span, jnp.concatenate([left_ref[row, s].T for s in span], axis=1)))
        for c0 in range(0, per, 2):
            columns = range(c0, min(c0 + 2, per))
            total = None
            for span, left in lefts:
                right = jnp.concatenate(
                    [jnp.concatenate([block(row, s, c) for c in columns], axis=1) for s in span],
                    axis=0,
                )
                term = jnp.dot(left, right, preferred_element_type=jnp.float32)
                total = term if total is None else total + term
            for c in columns:
                value = total[:, (c - c0) * size : (c - c0 + 1) * size]
                if coded:
                    codes = store_codes(out_ref, row, c, value, codes)
                else:
                    out_ref[row, c] = value
        if coded:
            out_ref[row, pl.ds(per * size, TAIL), :] = codes.astype(jnp.int32).astype(jnp.int16)


def product(tab, local_b, pieces, first, own, per, coded):
    slots, size = pieces[0].shape[1], pieces[0].shape[3]
    held = local_b.shape[1]
    if coded:
        out = jax.ShapeDtypeStruct((own, per * size + TAIL, size), jnp.int16)
    else:
        out = jax.ShapeDtypeStruct((own, per, size, size), jnp.float32)
    return pl.pallas_call(
        functools.partial(product_kernel, first, own, slots, per, size, coded, len(pieces)),
        out_shape=out,
        in_specs=[pl.BlockSpec(memory_space=pltpu.SMEM)]
        + [pl.BlockSpec(memory_space=pltpu.VMEM)] * (1 + len(pieces)),
        out_specs=pl.BlockSpec(memory_space=pltpu.VMEM),
        scratch_shapes=[pltpu.VMEM((own, slots, size, size), local_b.dtype)],
        compiler_params=pltpu.CompilerParams(vmem_limit_bytes=VMEM_LIMIT),
        cost_estimate=pl.CostEstimate(
            flops=2 * own * slots * per * size**3,
            bytes_accessed=own * slots * (held + 1) * size * size * 2 + own * per * size * size * 4,
            transcendentals=0,
        ),
        name="product_coded" if coded else "product_kept",
    )(tab, local_b.reshape(-1, size, size), *pieces)


def sum_kernel(per, size, coded, kept_ref, *refs):
    coded_refs, out_ref = refs[:-1], refs[-1]
    codes_in = [scales(ref, 0, per) for ref in coded_refs]
    codes = jnp.zeros((TAIL, size), jnp.float32)
    for c in range(per):
        value = kept_ref[0, c]
        for ref, code in zip(coded_refs, codes_in, strict=True):
            value = value + decode(ref, 0, c, code)
        if coded:
            codes = store_codes(out_ref, 0, c, value, codes)
        else:
            out_ref[0, c] = value
    if coded:
        out_ref[0, pl.ds(per * size, TAIL), :] = codes.astype(jnp.int32).astype(jnp.int16)


def combine(kept, arrived, coded):
    own, per, size, _ = kept.shape
    rows = per * size + TAIL
    kept_spec = pl.BlockSpec((1, per, size, size), lambda r: (r, 0, 0, 0))
    coded_spec = pl.BlockSpec((1, rows, size), lambda r: (r, 0, 0))
    out = jax.ShapeDtypeStruct((own, rows, size), jnp.int16) if coded else kept
    return pl.pallas_call(
        functools.partial(sum_kernel, per, size, coded),
        grid=(own,),
        out_shape=jax.ShapeDtypeStruct(out.shape, out.dtype),
        in_specs=[kept_spec] + [coded_spec] * len(arrived),
        out_specs=coded_spec if coded else kept_spec,
        compiler_params=pltpu.CompilerParams(vmem_limit_bytes=VMEM_LIMIT),
        cost_estimate=pl.CostEstimate(
            flops=own * rows * size * 4,
            bytes_accessed=own * rows * size * (4 + 2 * len(arrived) + 2),
            transcendentals=0,
        ),
        name="sum_coded" if coded else "sum_kept",
    )(kept, *arrived)


def settle_kernel(small_ref, out_ref):
    out_ref[...] = small_ref[...]


def settle(small):
    return pl.pallas_call(
        settle_kernel,
        out_shape=jax.ShapeDtypeStruct(small.shape, small.dtype),
        in_specs=[pl.BlockSpec(memory_space=pltpu.VMEM)],
        out_specs=pl.BlockSpec(memory_space=pltpu.VMEM),
        compiler_params=pltpu.CompilerParams(vmem_limit_bytes=VMEM_LIMIT),
        cost_estimate=pl.CostEstimate(flops=2 * 10**10, bytes_accessed=0, transcendentals=0),
        name="settle",
    )(small)


def gather_pieces(piece):
    extent = lax.axis_size("rep")
    outer, inner = split_two(extent)
    pieces = [piece]
    for step in range(1, outer):
        pieces.append(lax.ppermute(piece, "rep", routes(extent, step, 0)))
    if inner == 2:
        near = list(pieces)
        for p in near:
            pieces.append(lax.ppermute(p, "rep", routes(extent, 0, 1)))
    return pieces


def piece_order():
    extent = lax.axis_size("rep")
    outer, inner = split_two(extent)
    me = lax.axis_index("rep")
    o, i = me // inner, me % inner
    return [
        source(o, step, outer) * inner + (i ^ flip) for flip in range(inner) for step in range(outer)
    ]


def per_device(a_blocks, a_cols, b_blocks, b_cols, c_cols):
    own, _, slots, size, width = a_blocks.shape
    local_b, local_bcols, pattern = b_blocks[:, 0], b_cols[:, 0], c_cols[:, 0]
    held, per = local_b.shape[1], pattern.shape[1]
    extent = lax.axis_size("blk")
    outer, inner = split_two(extent)
    me = lax.axis_index("blk")
    o, i = me // inner, me % inner
    a_turned = jnp.swapaxes(a_blocks, 3, 4)

    def take_panel(panel):
        return lax.dynamic_index_in_dim(a_turned, panel, 1, keepdims=False)

    steps = list(range(1, outer))[::-1] + [0]
    order = [(k, j) for k in steps for j in reversed(range(inner))]

    arrived = {}
    for k, j in [(0, j) for j in reversed(range(inner))] + [x for x in order if x[0]]:
        sent = take_panel(partner(o, k, outer) * inner + (i ^ j))
        arrived[k, j] = lax.ppermute(sent, "blk", routes(extent, k, j)) if k or j else sent

    a_cols = settle(a_cols)
    slab_cols = lax.all_to_all(a_cols, "blk", split_axis=1, concat_axis=0, tiled=True)
    where_k = slab_cols.reshape(extent * own, slots)
    hits = local_bcols[where_k][:, :, :, None] == pattern[:, None, None, :]
    slot_t = jnp.arange(held, dtype=jnp.int32)[None, None, :, None]
    found = jnp.min(jnp.where(hits, slot_t, held), axis=2)
    at = jnp.where(found < held, where_k[:, :, None] * held + found, -1)
    table = jnp.concatenate([where_k, at.reshape(extent * own, slots * per)], axis=1)
    owners = jnp.stack([source(o, k, outer) * inner + (i ^ j) for k, j in order])
    table = table.reshape(extent, own, -1)[owners].reshape(extent * own, -1)
    places = piece_order()
    columns = max(table.shape[1], len(places))
    table = jnp.pad(table, ((0, 1), (0, columns - table.shape[1])))
    table = table.at[-1, : len(places)].set(jnp.stack(places).astype(jnp.int32))

    def ready(k, j):
        if width % 16 == 0:
            return gather_pieces(arrived[k, j])
        return [lax.all_gather(arrived[k, j], "rep", axis=2, tiled=True)]

    kept, arriving = {}, {k: [] for k in steps}
    for k in steps:
        for j in reversed(range(inner)):
            pieces = ready(k, j)
            done = product(table, local_b, pieces, order.index((k, j)) * own, own, per, coded=j > 0)
            if j:
                arriving[k].append(lax.ppermute(done, "blk", routes(extent, 0, j)))
            else:
                kept[k] = done
    for k in sorted(steps[:-1], key=lambda k: (hop(k, outer), -k)):
        summed = combine(kept[k], arriving[k], coded=True)
        step = hop(k, outer)
        arriving[k - step].append(lax.ppermute(summed, "blk", back_routes(extent, step)))
    mine = combine(kept[0], arriving[0], coded=False)
    return mine.reshape(own, 1, per, size, size)


def solution(mesh):
    placed = (
        P("blk", None, None, None, "rep"),
        P("blk", None, None),
        P("blk", "rep", None, None, None),
        P("blk", "rep", None),
        P(None, "rep", None),
    )
    return jax.shard_map(
        per_device,
        mesh=mesh,
        in_specs=placed,
        out_specs=P("blk", "rep", None, None, None),
        check_vma=False,
    )
```

```python
import functools

import jax
import jax.numpy as jnp
from jax import lax
from jax.experimental import pallas as pl
from jax.experimental.pallas import tpu as pltpu
from jax.sharding import PartitionSpec as P


LEVELS = 32600.0
STEPS = 256.0
TAIL = 16
VMEM_LIMIT = 12 * 1024 * 1024


def split_two(extent):
    inner = 2 if extent % 2 == 0 else 1
    return extent // inner, inner


def partner(index, step, extent):
    return index ^ step if extent & (extent - 1) == 0 else (index + step) % extent


def source(index, step, extent):
    return index ^ step if extent & (extent - 1) == 0 else (index + extent - step) % extent


def routes(extent, step, flip):
    outer, inner = split_two(extent)
    return [
        (o * inner + i, partner(o, step, outer) * inner + (i ^ flip))
        for o in range(outer)
        for i in range(inner)
    ]


def back_routes(extent, step):
    return [(to, frm) for frm, to in routes(extent, step, 0)]


def hop(step, extent):
    return step & -step if extent & (extent - 1) == 0 else step


def encode(values):
    top = jnp.max(jnp.abs(values), axis=0, keepdims=True)
    code = jnp.ceil(jnp.log2(jnp.maximum(top, 1e-33)) * STEPS)
    factor = jnp.exp2(code * (-1.0 / STEPS)) * LEVELS
    return jnp.round(values * factor).astype(jnp.int32).astype(jnp.int16), code


def store_codes(out_ref, row, column, values, codes):
    size = values.shape[1]
    coded, code = encode(values)
    out_ref[row, pl.ds(column * size, size), :] = coded
    line = lax.broadcasted_iota(jnp.int32, (TAIL, size), 0)
    return jnp.where(line == column, code, codes)


def decode(ref, row, column, codes):
    size = codes.shape[1]
    step = jnp.exp2(codes[column : column + 1] * (1.0 / STEPS)) * (1.0 / LEVELS)
    return ref[row, pl.ds(column * size, size), :].astype(jnp.int32).astype(jnp.float32) * step


def scales(ref, row, per):
    size = ref.shape[2]
    return ref[row, pl.ds(per * size, TAIL), :].astype(jnp.int32).astype(jnp.float32)


def product_kernel(group, own, slots, per, size, held, coded, pieces, meta_ref, has_ref, want_ref, b_ref, *refs):
    piece_refs, out_ref, left_ref = refs[:pieces], refs[pieces], refs[pieces + 1]
    width = (piece_refs[0].shape[0] - TAIL) // (own * slots)
    body = own * slots * width
    owner = meta_ref[group]
    places = meta_ref.shape[0] - pieces
    lines = piece_refs[0][pl.ds(body, TAIL), :].astype(jnp.float32).astype(jnp.int32)

    for n in range(pieces):
        at = pl.multiple_of(meta_ref[places + n] * width, width)
        piece = piece_refs[n][pl.ds(0, body), :]
        left_ref[:, :, pl.ds(at, width), :] = piece.reshape(own, slots, width, size)

    def found(row, s):
        k = lines[row, s]
        has = [has_ref[t, 0, k] for t in range(held)]
        out = []
        for c in range(per):
            want = want_ref[0, c, owner * own + row]
            at = jnp.int32(-1)
            for t in range(held):
                at = jnp.where(has[t] == want, k * held + t, at)
            out.append(at)
        return out

    def block(at):
        value = b_ref[jnp.maximum(at, 0)]
        return jnp.where(at >= 0, value, jnp.zeros_like(value))

    for row in range(own):
        codes = jnp.zeros((TAIL, size), jnp.float32)
        at = [found(row, s) for s in range(slots)]
        lefts = []
        for s0 in range(0, slots, 2):
            span = range(s0, min(s0 + 2, slots))
            lefts.append((span, jnp.concatenate([left_ref[row, s].T for s in span], axis=1)))
        for c0 in range(0, per, 2):
            columns = range(c0, min(c0 + 2, per))
            total = None
            for span, left in lefts:
                right = jnp.concatenate(
                    [jnp.concatenate([block(at[s][c]) for c in columns], axis=1) for s in span],
                    axis=0,
                )
                term = jnp.dot(left, right, preferred_element_type=jnp.float32)
                total = term if total is None else total + term
            for c in columns:
                value = total[:, (c - c0) * size : (c - c0 + 1) * size]
                if coded:
                    codes = store_codes(out_ref, row, c, value, codes)
                else:
                    out_ref[row, c] = value
        if coded:
            out_ref[row, pl.ds(per * size, TAIL), :] = codes.astype(jnp.int32).astype(jnp.int16)


def product(meta, has, want, blocks, pieces, group, own, slots, coded):
    size, held, per = blocks.shape[2], has.shape[0], want.shape[1]
    if coded:
        out = jax.ShapeDtypeStruct((own, per * size + TAIL, size), jnp.int16)
    else:
        out = jax.ShapeDtypeStruct((own, per, size, size), jnp.float32)
    return pl.pallas_call(
        functools.partial(
            product_kernel, group, own, slots, per, size, held, coded, len(pieces)
        ),
        out_shape=out,
        in_specs=[pl.BlockSpec(memory_space=pltpu.SMEM)] * 3
        + [pl.BlockSpec(memory_space=pltpu.VMEM)] * (1 + len(pieces)),
        out_specs=pl.BlockSpec(memory_space=pltpu.VMEM),
        scratch_shapes=[pltpu.VMEM((own, slots, size, size), blocks.dtype)],
        compiler_params=pltpu.CompilerParams(vmem_limit_bytes=VMEM_LIMIT),
        cost_estimate=pl.CostEstimate(
            flops=2 * own * slots * per * size**3,
            bytes_accessed=own * slots * (held + 1) * size * size * 2 + own * per * size * size * 4,
            transcendentals=0,
        ),
        name="product_coded" if coded else "product_kept",
    )(meta, has, want, blocks, *pieces)


def sum_kernel(per, size, coded, kept_ref, *refs):
    coded_refs, out_ref = refs[:-1], refs[-1]
    codes_in = [scales(ref, 0, per) for ref in coded_refs]
    codes = jnp.zeros((TAIL, size), jnp.float32)
    for c in range(per):
        value = kept_ref[0, c]
        for ref, code in zip(coded_refs, codes_in, strict=True):
            value = value + decode(ref, 0, c, code)
        if coded:
            codes = store_codes(out_ref, 0, c, value, codes)
        else:
            out_ref[0, c] = value
    if coded:
        out_ref[0, pl.ds(per * size, TAIL), :] = codes.astype(jnp.int32).astype(jnp.int16)


def combine(kept, arrived, coded):
    own, per, size, _ = kept.shape
    rows = per * size + TAIL
    kept_spec = pl.BlockSpec((1, per, size, size), lambda r: (r, 0, 0, 0))
    coded_spec = pl.BlockSpec((1, rows, size), lambda r: (r, 0, 0))
    out = jax.ShapeDtypeStruct((own, rows, size), jnp.int16) if coded else kept
    return pl.pallas_call(
        functools.partial(sum_kernel, per, size, coded),
        grid=(own,),
        out_shape=jax.ShapeDtypeStruct(out.shape, out.dtype),
        in_specs=[kept_spec] + [coded_spec] * len(arrived),
        out_specs=coded_spec if coded else kept_spec,
        compiler_params=pltpu.CompilerParams(vmem_limit_bytes=VMEM_LIMIT),
        cost_estimate=pl.CostEstimate(
            flops=own * rows * size * 4,
            bytes_accessed=own * rows * size * (4 + 2 * len(arrived) + 2),
            transcendentals=0,
        ),
        name="sum_coded" if coded else "sum_kept",
    )(kept, *arrived)


def pack_kernel(own, slots, count, meta_ref, cols_ref, a_ref, *out_refs):
    each, lanes = a_ref.shape[2], a_ref.shape[3]
    line = lax.broadcasted_iota(jnp.int32, (TAIL, lanes), 0)
    lane = lax.broadcasted_iota(jnp.int32, (TAIL, lanes), 1)
    for n in range(count):
        panel = meta_ref[count + n]
        tail = jnp.zeros((TAIL, lanes), jnp.int32)
        for row in range(own):
            out_refs[n][pl.ds(row * each, each), :] = a_ref[row, panel]
            for s in range(slots):
                tail = jnp.where((line == row) & (lane == s), cols_ref[row, panel, s], tail)
        out_refs[n][pl.ds(own * each, TAIL), :] = tail.astype(jnp.float32).astype(a_ref.dtype)


def pack(meta, a_turned, cols):
    own, count, each, size = a_turned.shape
    return pl.pallas_call(
        functools.partial(pack_kernel, own, cols.shape[2], count),
        out_shape=[jax.ShapeDtypeStruct((own * each + TAIL, size), a_turned.dtype)] * count,
        in_specs=[pl.BlockSpec(memory_space=pltpu.SMEM)] * 2
        + [pl.BlockSpec(memory_space=pltpu.VMEM)],
        out_specs=[pl.BlockSpec(memory_space=pltpu.VMEM)] * count,
        compiler_params=pltpu.CompilerParams(vmem_limit_bytes=VMEM_LIMIT),
        cost_estimate=pl.CostEstimate(flops=6 * 10**9, bytes_accessed=2 * 10**7, transcendentals=0),
        name="pack",
    )(meta, cols, a_turned)


def gather_pieces(piece):
    extent = lax.axis_size("rep")
    outer, inner = split_two(extent)
    pieces = [piece]
    for step in range(1, outer):
        pieces.append(lax.ppermute(piece, "rep", routes(extent, step, 0)))
    if inner == 2:
        near = list(pieces)
        for p in near:
            pieces.append(lax.ppermute(p, "rep", routes(extent, 0, 1)))
    return pieces


def piece_order():
    extent = lax.axis_size("rep")
    outer, inner = split_two(extent)
    me = lax.axis_index("rep")
    o, i = me // inner, me % inner
    return [
        source(o, step, outer) * inner + (i ^ flip) for flip in range(inner) for step in range(outer)
    ]


def per_device(a_blocks, a_cols, b_blocks, b_cols, c_cols):
    own, panels, slots, size, width = a_blocks.shape
    local_b, per = b_blocks[:, 0], c_cols.shape[2]
    assert local_b.shape[0] <= 256
    extent = lax.axis_size("blk")
    outer, inner = split_two(extent)
    me = lax.axis_index("blk")
    o, i = me // inner, me % inner
    steps = list(range(1, outer))[::-1] + [0]
    order = [(k, j) for k in steps for j in reversed(range(inner))]

    whole = width % 16 != 0
    owners = [source(o, k, outer) * inner + (i ^ j) for k, j in order]
    to = [partner(o, k, outer) * inner + (i ^ j) for k, j in order]
    places = [jnp.int32(0)] if whole else piece_order()
    meta = jnp.stack([x.astype(jnp.int32) for x in owners + to + places])
    has, want = jnp.transpose(b_cols, (2, 1, 0)), jnp.transpose(c_cols, (1, 2, 0))
    blocks = local_b.reshape(-1, size, size)

    a_turned = jnp.swapaxes(a_blocks, 3, 4).reshape(own, panels, slots * width, size)
    messages = pack(meta, a_turned, a_cols)
    arrived = {}
    for (k, j), sent in zip(order, messages, strict=True):
        arrived[k, j] = lax.ppermute(sent, "blk", routes(extent, k, j)) if k or j else sent

    def ready(k, j):
        if not whole:
            return gather_pieces(arrived[k, j])
        body = arrived[k, j][:-TAIL].reshape(own, slots, width, size)
        body = lax.all_gather(body, "rep", axis=2, tiled=True).reshape(-1, size)
        return [jnp.concatenate([body, arrived[k, j][-TAIL:]], axis=0)]

    kept, arriving = {}, {k: [] for k in steps}
    for k in steps:
        for j in reversed(range(inner)):
            pieces = ready(k, j)
            done = product(meta, has, want, blocks, pieces, order.index((k, j)), own, slots, j > 0)
            if j:
                arriving[k].append(lax.ppermute(done, "blk", routes(extent, 0, j)))
            else:
                kept[k] = done
    for k in sorted(steps[:-1], key=lambda k: (hop(k, outer), -k)):
        summed = combine(kept[k], arriving[k], coded=True)
        step = hop(k, outer)
        arriving[k - step].append(lax.ppermute(summed, "blk", back_routes(extent, step)))
    mine = combine(kept[0], arriving[0], coded=False)
    return mine.reshape(own, 1, per, size, size)


def solution(mesh):
    placed = (
        P("blk", None, None, None, "rep"),
        P("blk", None, None),
        P("blk", "rep", None, None, None),
        P("blk", "rep", None),
        P(None, "rep", None),
    )
    return jax.shard_map(
        per_device,
        mesh=mesh,
        in_specs=placed,
        out_specs=P("blk", "rep", None, None, None),
        check_vma=False,
    )
```
